1024 devices in a mesh: wide: 64 (over x, y, core), narrow: 16 (over z).
Axes of the slice: x: 4, y: 8, z: 16, core: 2. Of those that a mesh axis runs over, the one named last changes fastest.
Arguments:
- tokens: bfloat16 [1536, 4096], P('wide', 'narrow'), may hold values from -6 to 6
- grad_out: bfloat16 [1536, 4096], P('wide', 'narrow'), may hold values from -1.1953125 to 1.1953125
- expert_ids: int32 [1536, 8], P('wide'), may hold values from 0 to 63, all different within a row; in each aligned block of 24 rows (0 to 23, 24 to 47, ...) at most 6 rows name the same one
- route_weights: bfloat16 [1536, 8], P('wide'), may hold values from 0.049804688 to 1
- w_gate: bfloat16 [64, 4096, 1536], P('wide', None, 'narrow'), may hold values from -0.09375 to 0.09375
- w_up: bfloat16 [64, 4096, 1536], P('wide', None, 'narrow'), may hold values from -0.09375 to 0.09375
- w_down: bfloat16 [64, 1536, 4096], P('wide', 'narrow'), may hold values from -0.15625 to 0.15625
Outputs:
- grad_tokens: bfloat16 [1536, 4096], P('wide', 'narrow')
- grad_route: bfloat16 [1536, 8], P('wide')
- grad_down: bfloat16 [64, 1536, 4096], P('wide', 'narrow')
The draws below stay inside these ranges and needn't reach their ends.
Inputs may be any that keep to these rules, and one draw needn't show every extreme that they name: `expert_ids`: each row names 8 different experts. In each aligned block of 24 rows (the tokens of one index of wide) no expert is named by more than 6 rows, a bound that some block reaches.
All inputs are finite; a program needn't handle non-finite values.
Results may differ from the reference program's by a relative error of at most 0.019.
Values may be sent and summed in bfloat16 or wider, within the bound.
A program may use at most 32 MiB of HBM per device.

```python
import math
import jax
import jax.numpy as jnp
import numpy as np
from jax import lax

D = 4096
FF = 1536
TOP = 8
TOK_COL = 24
EXPERTS = 64
CAP = 6
TOKENS = 1536
N_WIDE = 64
N_NARROW = 16


def levels(rng, shape, pieces, smallest, largest):
    def one(dim, blocks):
        draws = jax.random.uniform(jax.random.fold_in(jax.random.fold_in(rng, 6), dim), (blocks,), jnp.float32, smallest / len(pieces), largest / len(pieces))
        return jnp.repeat(jnp.exp(draws), shape[dim] // blocks).reshape((-1,) + (1,) * (len(shape) - dim - 1))

    factor_of = one(*pieces[0])
    for cut in pieces[1:]:
        factor_of = factor_of * one(*cut)
    return factor_of


def routed_block(stream_key, own, number, rows, count, top, reach, lean):
    sequence = jax.random.permutation(stream_key, count)
    heavy_load, common = load_shares(count, rows * top, reach, lean, True), load_shares(count, rows * top, reach, lean, False)
    places = jnp.arange(count)

    def named(tallies, offset_by):
        used = int((tallies > 0).sum())
        fixed = max(1, used // 4)
        passed = fixed + (places - fixed + offset_by * (used - fixed)) % max(1, count - fixed)
        return jnp.zeros((count,), jnp.int32).at[sequence[jnp.where(places < fixed, places, passed)]].set(jnp.asarray(tallies, jnp.int32))

    tallies = jnp.where(number % 4 == 0, named(heavy_load, number // 4), named(common, number - number // 4 - 1))
    mixed = jax.random.permutation(jax.random.fold_in(own, 3), count)
    giver, receiver = mixed[0:count // 2 * 2:2], mixed[1:count // 2 * 2:2]
    room = jnp.minimum(tallies[giver] - 1, reach - tallies[receiver]) // 2
    room = jnp.where((giver == sequence[0]) | (receiver == sequence[0]) | (tallies[receiver] == 0), 0, jnp.maximum(room, 0))
    passed = jax.random.randint(jax.random.fold_in(own, 4), (count // 2,), 0, 1 << 20) % (room + 1)
    tallies = tallies.at[giver].add(-passed).at[receiver].add(passed)
    items = jnp.searchsorted(jnp.cumsum(tallies), jnp.arange(rows * top), side="right").astype(jnp.int32)
    table = items.reshape(top, rows).T
    table = table[jax.random.permutation(jax.random.fold_in(own, 1), rows)]
    offset_by = jax.random.randint(jax.random.fold_in(own, 2), (rows, 1), 0, top)
    return jnp.take_along_axis(table, (jnp.arange(top)[None, :] + offset_by) % top, axis=1)


def load_shares(amount, total, limit, lean, full):
    loads = [(1 << 20) // math.isqrt(rank ** lean) + 1 for rank in range(1, amount + 1)]
    largest = limit if full else min(limit, max(-(-total // amount), total * loads[0] // sum(loads)))
    least = 1 if total - largest >= amount - 1 else 0
    given, spare = [largest] + [least] * (amount - 1), total - largest - least * (amount - 1)
    while spare > 0:
        free = [i for i in range(1, amount) if given[i] < largest] or [i for i in range(1, amount) if given[i] < limit]
        pool, budget = sum([loads[i] for i in free]), spare
        for i in free:
            more = min(limit - given[i], max(1, budget * loads[i] // pool), spare)
            given[i] = given[i] + more
            spare = spare - more
    return np.array(given)


def noise(rng, dims, scale, most, pieces=(), kind=jnp.bfloat16):
    result = jax.random.normal(rng, dims, jnp.float32) * scale
    if len(pieces) > 0:
        result = levels(rng, dims, pieces, -0.22, 0.18) * result
    return jnp.clip(result, min=-most, max=most).astype(kind)


def setup_inputs(seed: int = 0) -> dict:
    keys = jax.random.split(jax.random.key(seed), 8)
    tokens = noise(keys[0], (TOKENS, D), 1.0, 6.0, ((0, 64), (1, 16)))
    grad_out = noise(keys[1], (TOKENS, D), 0.2, 1.1953125, ((0, 64), (1, 16)))
    expert_ids_keys = jax.random.split(jax.random.fold_in(keys[2], 1), TOKENS // TOK_COL)
    expert_ids_turns = jax.random.permutation(jax.random.fold_in(keys[2], 3), TOKENS // TOK_COL)
    expert_ids = jax.vmap(lambda own, number: routed_block(jax.random.fold_in(keys[2], 2), own, number, TOK_COL, EXPERTS, TOP, CAP, 2))(expert_ids_keys, expert_ids_turns).reshape((TOKENS, TOP))
    route_weights = jnp.clip(jnp.exp(math.log(1.0) - 2.9996462 * jax.random.uniform(keys[3], (TOKENS, TOP), jnp.float32) ** levels(keys[3], (TOKENS, TOP), ((0, 64),), -0.2, 0.2)), 0.049804688, 1.0).astype(jnp.bfloat16)
    w_gate = noise(keys[4], (EXPERTS, D, FF), D ** -0.5, 0.09375, ((0, 64), (2, 16)))
    w_up = noise(keys[5], (EXPERTS, D, FF), D ** -0.5, 0.09375, ((0, 64), (2, 16)))
    w_down = noise(keys[6], (EXPERTS, FF, D), FF ** -0.5, 0.15625, ((0, 64), (1, 16)))
    return dict(tokens=tokens, grad_out=grad_out, expert_ids=expert_ids, route_weights=route_weights, w_gate=w_gate, w_up=w_up, w_down=w_down)


def silu_parts(gate_pre):
    sigmoid_val = jax.nn.sigmoid(gate_pre)
    return gate_pre * sigmoid_val, sigmoid_val * (1.0 + gate_pre * (1.0 - sigmoid_val))


def reference(tokens, grad_out, expert_ids, route_weights, w_gate, w_up, w_down):
    slot_rows = N_WIDE * CAP
    copies = TOK_COL * TOP
    blocks = expert_ids.reshape(N_WIDE, copies)
    onehot = (blocks[:, :, None] == jnp.arange(EXPERTS, dtype=jnp.int32)[None, None, :]).astype(jnp.int32)
    before = jnp.cumsum(onehot, axis=1) - onehot
    rank_in = jnp.sum(before * onehot, axis=2)
    column = jnp.arange(N_WIDE, dtype=jnp.int32)[:, None]
    position = (blocks * slot_rows + column * CAP + rank_in).reshape(-1).astype(jnp.int32)
    copy_index = jnp.arange(N_WIDE * copies, dtype=jnp.int32)
    token_index = (copy_index // TOP).astype(jnp.int32)
    token_table = jnp.zeros((EXPERTS * slot_rows,), jnp.int32).at[position].set(token_index).reshape(EXPERTS, slot_rows)
    copy_table = jnp.zeros((EXPERTS * slot_rows,), jnp.int32).at[position].set(copy_index).reshape(EXPERTS, slot_rows)
    filled = jnp.zeros((EXPERTS * slot_rows,), jnp.float32).at[position].set(1.0).reshape(EXPERTS, slot_rows)
    weight_flat = route_weights.reshape(-1).astype(jnp.float32)
    width = FF // N_NARROW

    def expert(operands):
        gate_w, up_w, down_w, token_idx, copy_idx, filled_row = operands
        keep_row = filled_row[:, None] > 0
        token_rows = jnp.where(keep_row, tokens[token_idx], jnp.zeros((), tokens.dtype))
        grad_rows = jnp.where(keep_row, grad_out[token_idx], jnp.zeros((), grad_out.dtype))
        gain_rows = weight_flat[copy_idx] * filled_row
        gate_pre = jnp.dot(token_rows, gate_w, preferred_element_type=jnp.float32)
        up_pre = jnp.dot(token_rows, up_w, preferred_element_type=jnp.float32)
        active, gate_slope = silu_parts(gate_pre)
        hidden = (active * up_pre).astype(jnp.bfloat16)
        back_proj = jnp.dot(grad_rows, down_w.T, preferred_element_type=jnp.float32)
        d_hidden = gain_rows[:, None] * back_proj
        d_gate = (d_hidden * up_pre * gate_slope).astype(jnp.bfloat16)
        d_up = (d_hidden * active).astype(jnp.bfloat16)
        scaled = (gain_rows[:, None] * grad_rows.astype(jnp.float32)).astype(jnp.bfloat16)
        grad_down = jnp.dot(hidden.T, scaled, preferred_element_type=jnp.float32).astype(jnp.bfloat16)
        input_total = jnp.zeros((slot_rows, D), jnp.float32)
        route_total = jnp.zeros((slot_rows,), jnp.float32)
        for block_id in range(N_NARROW):
            low = block_id * width
            high = low + width
            part_in = jnp.dot(d_gate[:, low:high], gate_w[:, low:high].T, preferred_element_type=jnp.float32)
            part_in = part_in + jnp.dot(d_up[:, low:high], up_w[:, low:high].T, preferred_element_type=jnp.float32)
            input_total = input_total + lax.optimization_barrier(part_in.astype(jnp.bfloat16)).astype(jnp.float32)
            part_route = jnp.sum(hidden[:, low:high].astype(jnp.float32) * back_proj[:, low:high], axis=1)
            route_total = route_total + lax.optimization_barrier(part_route.astype(jnp.bfloat16)).astype(jnp.float32)
        return grad_down, input_total.astype(jnp.bfloat16), route_total.astype(jnp.bfloat16)

    grad_down, input_rows, route_rows = lax.map(
        expert, (w_gate, w_up, w_down, token_table, copy_table, filled))
    flat_filled = filled.reshape(-1)
    grad_tokens = jnp.zeros((TOKENS, D), jnp.float32).at[token_table.reshape(-1)].add(
        input_rows.reshape(-1, D).astype(jnp.float32) * flat_filled[:, None])
    grad_route = jnp.zeros((TOKENS * TOP,), jnp.float32).at[copy_table.reshape(-1)].add(
        route_rows.reshape(-1).astype(jnp.float32) * flat_filled)
    return (grad_tokens.astype(jnp.bfloat16), grad_route.reshape(TOKENS, TOP).astype(jnp.bfloat16),
            grad_down)
```

```python
import functools

import jax
import jax.numpy as jnp
from jax import lax
from jax.experimental import pallas as pl
from jax.experimental.pallas import tpu as pltpu
from jax.sharding import PartitionSpec as P

MESH = pl.DeviceIdType.MESH
F32 = jnp.float32
BF16 = jnp.bfloat16
LANES = 128


def dot_nn(a, b):
    return lax.dot_general(a, b, (((1,), (0,)), ((), ())), preferred_element_type=F32)


def dot_nt(a, b):
    return lax.dot_general(a, b, (((1,), (1,)), ((), ())), preferred_element_type=F32)


def dot_tn(a, b):
    return lax.dot_general(a, b, (((0,), (0,)), ((), ())), preferred_element_type=F32)


def steps_of(value, width, count):
    out = jnp.zeros_like(value)
    for m in range(1, count):
        out = out + (value >= width * m).astype(jnp.int32)
    return out


def kernel(
    cfg,
    ids_ref,
    rw_ref,
    tok_ref,
    grd_ref,
    wg_ref,
    wu_ref,
    wd_ref,
    gtok_out,
    groute_out,
    gdown_out,
    pack,
    ycol,
    place_t,
    emat,
    slot_key,
    sel,
    gtok,
    ggrd,
    gain,
    wgu,
    wdn,
    acc_gu,
    acc_bp,
    dcat,
    hidden,
    rs_send,
    rs_recv,
    zroute,
    zroute_own,
    rsum,
    xroute,
    cgrad,
    xback,
    yback_send,
    yback,
    gdown,
    y_snd,
    y_rcv,
    x_snd,
    x_rcv,
    g_snd,
    g_rcv,
    r_snd,
    r_rcv,
    z_snd,
    z_rcv,
    xb_snd,
    xb_rcv,
    yb_snd,
    yb_rcv,
    w_sem,
    o_sem,
):
    X, Y, C, Z = cfg["X"], cfg["Y"], cfg["C"], cfg["Z"]
    T, TP, F, H, HP, E, TOP, CAP = (
        cfg[k] for k in ("T", "TP", "F", "H", "HP", "E", "TOP", "CAP")
    )
    NP = X * C
    PB = Y * CAP
    SLOTS = NP * PB
    TOKS = Y * TP
    half = Z // 2
    A = F // 2

    w = lax.axis_index("wide")
    z = lax.axis_index("narrow")
    x = w // (Y * C)
    y = (w // C) % Y
    c = w % C
    me = x * C + c

    def y_peer(d):
        yy = (y + d) % Y
        return yy, (x * (Y * C) + yy * C + c, z)

    def x_peer(d):
        p = (me + d) % NP
        return p, ((p // C) * (Y * C) + y * C + p % C, z)

    right = (w, (z + 1) % Z)
    left = (w, (z + Z - 1) % Z)

    def rows(block, size):
        return pl.ds(pl.multiple_of(block * size, 16), size)

    def cols(block):
        return pl.ds(pl.multiple_of(block * F, LANES), F)

    def remote(src, dst, snd, rcv, device):
        return pltpu.make_async_remote_copy(
            src_ref=src, dst_ref=dst, send_sem=snd, recv_sem=rcv, device_id=device, device_id_type=MESH
        )

    def each(first, last, body):
        lax.fori_loop(first, last, lambda i, carry: (body(i), carry)[1], 0)

    weights = [
        pltpu.make_async_copy(wg_ref, wgu.at[pl.ds(0, H), :], w_sem.at[0]),
        pltpu.make_async_copy(wu_ref, wgu.at[pl.ds(HP, H), :], w_sem.at[1]),
        pltpu.make_async_copy(wd_ref, wdn.at[pl.ds(0, H), :], w_sem.at[2]),
    ]
    for copy in weights:
        copy.start()

    barrier = pltpu.get_barrier_semaphore()

    def greet(device):
        pl.semaphore_signal(barrier, inc=1, device_id=device, device_id_type=MESH)

    each(1, Y, lambda d: greet(y_peer(d)[1]))
    each(1, NP, lambda d: greet(x_peer(d)[1]))
    each(1, Z, lambda d: greet((w, (z + d) % Z)))

    lane = lax.broadcasted_iota(jnp.int32, (TP, LANES), 1)
    lane_expert = jnp.where(lane >= E, lane - E, lane)
    named = jnp.zeros((TP, LANES), F32)
    weight = jnp.zeros((TP, LANES), F32)
    for k in range(TOP):
        hit = ids_ref[:, k : k + 1] == lane_expert
        named = named + jnp.where(hit, 1.0, 0.0)
        weight = weight + jnp.where(hit, rw_ref[:, k : k + 1], 0.0)
    tri = (
        lax.broadcasted_iota(jnp.int32, (TP, TP), 0) > lax.broadcasted_iota(jnp.int32, (TP, TP), 1)
    ).astype(F32)
    before = dot_nn(tri.astype(BF16), named.astype(BF16))
    table = jnp.where(lane < E, named * (before + 1.0), jnp.where(lane < 2 * E, weight, 0.0))

    pack[...] = jnp.zeros_like(pack)
    pack[0:T, 0:F] = tok_ref[...]
    pack[:, F : F + LANES] = table.astype(BF16)
    pack[0:T, F + LANES :] = grd_ref[...]

    pl.semaphore_wait(barrier, (Y - 1) + (NP - 1) + (Z - 1))

    parts = (pl.ds(0, F + LANES), pl.ds(F + LANES, F))

    def y_copy(part, d, owner, device):
        return remote(
            pack.at[:, parts[part]],
            ycol.at[rows(owner, TP), parts[part]],
            y_snd.at[part, d],
            y_rcv.at[part, d],
            device,
        )

    for part in range(2):
        each(1, Y, lambda d, part=part: y_copy(part, d, y, y_peer(d)[1]).start())
    ycol[rows(y, TP), :] = pack[...]

    slot = lax.broadcasted_iota(jnp.int32, (SLOTS, LANES), 0)
    slot_lane = lax.broadcasted_iota(jnp.int32, (SLOTS, LANES), 1)
    peer = steps_of(slot, PB, NP)
    peer_x = steps_of(peer, C, X)
    expert = peer_x * (Y * C) + y * C + (peer - peer_x * C)
    emat[0] = (slot_lane == expert).astype(F32).astype(BF16)
    emat[1] = (slot_lane == expert + E).astype(F32).astype(BF16)
    slot = lax.broadcasted_iota(jnp.int32, (SLOTS, TOKS), 0)
    tok_y = steps_of(lax.broadcasted_iota(jnp.int32, (SLOTS, TOKS), 1), TP, Y)
    inner = slot - PB * steps_of(slot, PB, NP)
    slot_y = steps_of(inner, CAP, Y)
    slot_key[...] = jnp.where(tok_y == slot_y, inner - CAP * slot_y + 1, -1).astype(F32)

    wgu[H:HP, :] = jnp.zeros((HP - H, wgu.shape[1]), BF16)
    wgu[HP + H :, :] = jnp.zeros((HP - H, wgu.shape[1]), BF16)
    wdn[H:, :] = jnp.zeros((HP - H, wdn.shape[1]), BF16)

    def y_wait(part):
        each(1, Y, lambda d: y_copy(part, d, (y + Y - d) % Y, y_peer(d)[1]).wait_recv())

    y_wait(0)
    tables = ycol[:, F : F + LANES]
    place = dot_nt(emat[0], tables) == slot_key[...]
    place_b = place.astype(F32).astype(BF16)
    sel[:, 0:F] = dot_nn(place_b, ycol[:, 0:F]).astype(BF16)

    def x_copy(part, d, src, dst, device):
        if part == 0:
            return remote(
                sel.at[rows(src, PB), pl.ds(0, F)],
                gtok.at[z, rows(dst, PB), :],
                x_snd.at[0, d],
                x_rcv.at[0, d],
                device,
            )
        if part == 1:
            return remote(
                sel.at[rows(src, PB), pl.ds(F, F)],
                ggrd.at[z, rows(dst, PB), :],
                x_snd.at[1, d],
                x_rcv.at[1, d],
                device,
            )
        return remote(
            sel.at[rows(src, PB), pl.ds(2 * F, LANES)],
            gain.at[rows(dst, PB), :],
            x_snd.at[2, d],
            x_rcv.at[2, d],
            device,
        )

    def x_start(part):
        def one(d):
            p, device = x_peer(d)
            x_copy(part, d, p, me, device).start()

        each(1, NP, one)

    def x_wait(part):
        def one(d):
            p = (me + NP - d) % NP
            x_copy(part, d, p, p, x_peer(d)[1]).wait_recv()

        each(1, NP, one)

    x_start(0)
    gtok[z, rows(me, PB), :] = sel[rows(me, PB), 0:F]

    y_wait(1)
    sel[:, F : 2 * F] = dot_nn(place_b, ycol[:, F + LANES :]).astype(BF16)
    x_start(1)
    weights_of = jnp.where(place, dot_nt(emat[1], tables), 0.0)
    sel[:, 2 * F :] = jnp.broadcast_to(
        jnp.sum(weights_of, axis=1, keepdims=True), (SLOTS, LANES)
    ).astype(BF16)
    x_start(2)
    ggrd[z, rows(me, PB), :] = sel[rows(me, PB), F : 2 * F]
    gain[rows(me, PB), :] = sel[rows(me, PB), 2 * F :]

    def hop(stream, s, sending):
        to_right = stream % 2 == 0
        buf = gtok if stream < 2 else ggrd
        back = s if sending else s + 1
        owner = (z + Z - back) % Z if to_right else (z + back) % Z
        return remote(
            buf.at[owner],
            buf.at[owner],
            g_snd.at[stream, s],
            g_rcv.at[stream, s],
            right if to_right else left,
        )

    def use_tokens(owner):
        acc_gu[...] += dot_nt(gtok[owner], wgu[:, cols(owner)])

    def use_grads(owner):
        acc_bp[...] += dot_nt(ggrd[owner], wdn[:, cols(owner)])

    x_wait(0)
    hop(0, 0, True).start()
    hop(1, 0, True).start()
    acc_gu[...] = jnp.zeros_like(acc_gu)
    acc_bp[...] = jnp.zeros_like(acc_bp)
    x_wait(1)
    hop(2, 0, True).start()
    hop(3, 0, True).start()
    for copy in weights:
        copy.wait()
    use_tokens(z)
    use_grads(z)

    key_slot = lax.broadcasted_iota(jnp.int32, (TOKS, SLOTS), 1)
    key_inner = key_slot - PB * steps_of(key_slot, PB, NP)
    key_y = steps_of(key_inner, CAP, Y)
    key_tok = steps_of(lax.broadcasted_iota(jnp.int32, (TOKS, SLOTS), 0), TP, Y)
    key = jnp.where(key_tok == key_y, key_inner - CAP * key_y + 1, -1).astype(F32)
    place_t[...] = (dot_nt(ycol[:, F : F + LANES], emat[0]) == key).astype(F32).astype(BF16)
    x_wait(2)

    def gather_step(s):
        hop(0, s - 1, False).wait_recv()
        hop(0, s, True).start()
        hop(1, s - 1, False).wait_recv()

        @pl.when(s < half - 1)
        def _():
            hop(1, s, True).start()

        hop(2, s - 1, False).wait_recv()

        @pl.when(s < half - 1)
        def _():
            hop(2, s, True).start()

        hop(3, s - 1, False).wait_recv()
        hop(3, s, True).start()
        use_tokens((z + Z - s) % Z)
        use_tokens((z + s) % Z)
        use_grads((z + Z - s) % Z)
        use_grads((z + s) % Z)

    each(1, half, gather_step)
    hop(0, half - 1, False).wait_recv()
    use_tokens((z + half) % Z)
    hop(3, half - 1, False).wait_recv()
    use_grads((z + half) % Z)

    gate = acc_gu[:, 0:HP]
    up = acc_gu[:, HP:]
    back = acc_bp[...]
    scale = gain[...].astype(F32)
    sig = jax.nn.sigmoid(gate)
    active = gate * sig
    slope = sig * (1.0 + gate * (1.0 - sig))
    hid = (active * up).astype(BF16)
    hidden[...] = hid
    d_hidden = scale * back
    dcat[:, 0:HP] = (d_hidden * up * slope).astype(BF16)
    dcat[:, HP:] = (d_hidden * active).astype(BF16)
    route = jnp.sum(hid.astype(F32) * back, axis=1, keepdims=True)

    def ring(stream, k):
        return remote(
            rs_send.at[stream, k],
            rs_recv.at[stream, k],
            r_snd.at[stream, k],
            r_rcv.at[stream, k],
            right if stream < 2 else left,
        )

    def partial(owner):
        return dot_nn(dcat[...], wgu[:, cols(owner)])

    def push(stream, k, value, add):
        if add:
            ring(stream, k + 1).wait_recv()
            value = value + rs_recv[stream, k + 1].astype(F32)
        rs_send[stream, k] = value.astype(BF16)
        ring(stream, k).start()

    def down(chunk):
        scaled = (jnp.concatenate([scale_ref()] * (F // LANES), axis=1) * ggrd[chunk].astype(F32)).astype(BF16)
        gdown[:, cols(chunk)] = dot_tn(hidden[...], scaled)[0:H, :].astype(BF16)

    def scale_ref():
        return gain[...].astype(F32)

    far = partial((z + half) % Z)
    push(0, half, far[:, 0:A], False)
    push(3, half, far[:, A:], False)
    to_right = partial((z + half - 1) % Z)
    to_left = partial((z + Z - half + 1) % Z)
    push(1, half - 1, to_right[:, A:], False)
    push(2, half - 1, to_left[:, 0:A], False)

    rt_row = lax.broadcasted_iota(jnp.int32, (SLOTS, LANES), 0)
    rt_inner = rt_row - PB * steps_of(rt_row, PB, NP)
    rt_lane = lax.broadcasted_iota(jnp.int32, (SLOTS, LANES), 1)
    spread = jnp.where(rt_lane == rt_inner, route.astype(BF16).astype(F32), 0.0).astype(BF16)
    blk = lax.broadcasted_iota(jnp.int32, (8, SLOTS), 0)
    blk_of = steps_of(lax.broadcasted_iota(jnp.int32, (8, SLOTS), 1), PB, NP)
    pick = (blk == blk_of).astype(F32).astype(BF16)
    zroute_own[...] = dot_nn(pick, spread)

    def z_copy(d, slot_d, device):
        return remote(zroute_own, zroute.at[slot_d], z_snd.at[d], z_rcv.at[d], device)

    each(1, Z, lambda d: z_copy(d, d, (w, (z + d) % Z)).start())

    push(0, half - 1, to_right[:, 0:A], True)
    push(3, half - 1, to_left[:, A:], True)
    for chunk in range(2):
        down(chunk)

    def reduce_step(i):
        k = half - 1 - i
        to_right = partial((z + k) % Z)
        to_left = partial((z + Z - k) % Z)
        push(0, k, to_right[:, 0:A], True)
        push(3, k, to_left[:, A:], True)
        push(1, k, to_right[:, A:], True)
        push(2, k, to_left[:, 0:A], True)
        per = -(-(Z - 2) // (half - 2))
        for j in range(per):
            chunk = 2 + (i - 1) * per + j

            @pl.when(chunk < Z)
            def _():
                down(chunk)

    each(1, half - 1, reduce_step)
    out_copy = pltpu.make_async_copy(gdown, gdown_out, o_sem)
    out_copy.start()

    each(1, Z, lambda d: z_copy(d, d, (w, (z + d) % Z)).wait_recv())
    total = zroute_own[...]
    for d in range(1, Z):
        total = total + zroute[d]
    rsum[...] = total.astype(BF16).astype(F32)

    def xb_copy(part, d, src, dst, device):
        if part == 0:
            return remote(rsum, xroute.at[dst], xb_snd.at[0, d], xb_rcv.at[0, d], device)
        return remote(
            cgrad.at[rows(src, PB), :],
            xback.at[rows(dst, PB), :],
            xb_snd.at[1, d],
            xb_rcv.at[1, d],
            device,
        )

    def xb_start(part):
        def one(d):
            p, device = x_peer(d)
            xb_copy(part, d, p, me, device).start()

        each(1, NP, one)

    def xb_wait(part):
        def one(d):
            p = (me + NP - d) % NP
            xb_copy(part, d, p, p, x_peer(d)[1]).wait_recv()

        each(1, NP, one)

    xb_start(0)
    xroute[me] = rsum[...]

    own = partial(z)
    for lanes, streams in ((slice(0, A), (0, 2)), (slice(A, F), (1, 3))):
        value = own[:, lanes]
        for stream in streams:
            ring(stream, 1).wait_recv()
            value = value + rs_recv[stream, 1].astype(F32)
        cgrad[:, lanes] = value.astype(BF16)
    xb_start(1)
    xback[rows(me, PB), :] = cgrad[rows(me, PB), :]

    xb_wait(0)
    sub = lax.broadcasted_iota(jnp.int32, (NP, 8, LANES), 1)
    mine = jnp.sum(jnp.where(sub == me, xroute[...], 0.0), axis=1).astype(BF16)
    lane_in = lax.broadcasted_iota(jnp.int32, (LANES, SLOTS), 0)
    slot_in = lax.broadcasted_iota(jnp.int32, (LANES, SLOTS), 1)
    slot_in = slot_in - PB * steps_of(slot_in, PB, NP)
    wide_rows = dot_nn(mine, (lane_in == slot_in).astype(F32).astype(BF16))
    from_peer = lax.broadcasted_iota(jnp.int32, (NP, SLOTS), 0)
    slot_peer = steps_of(lax.broadcasted_iota(jnp.int32, (NP, SLOTS), 1), PB, NP)
    values = jnp.sum(jnp.where(from_peer == slot_peer, wide_rows, 0.0), axis=0, keepdims=True)
    routed = (place_t[...].astype(F32) * values).astype(BF16)
    yback_send[:, F:] = dot_nn(routed, emat[0]).astype(BF16)

    xb_wait(1)
    yback_send[:, 0:F] = dot_nn(place_t[...], xback[...]).astype(BF16)

    def yb_copy(d, src, dst, device):
        return remote(
            yback_send.at[rows(src, TP), :], yback.at[rows(dst, TP), :], yb_snd.at[d], yb_rcv.at[d], device
        )

    def yb_start(d):
        yy, device = y_peer(d)
        yb_copy(d, yy, y, device).start()

    each(1, Y, yb_start)
    yback[rows(y, TP), :] = yback_send[rows(y, TP), :]

    def yb_wait(d):
        yy = (y + Y - d) % Y
        yb_copy(d, yy, yy, y_peer(d)[1]).wait_recv()

    each(1, Y, yb_wait)
    final = jnp.zeros((TP, F + LANES), F32)
    for j in range(Y):
        final = final + yback[j * TP : (j + 1) * TP, :].astype(F32)
    gtok_out[...] = final[0:T, 0:F].astype(BF16)
    per_expert = final[:, F:]
    out_lane = lax.broadcasted_iota(jnp.int32, (TP, TOP), 1)
    result = jnp.zeros((TP, TOP), F32)
    for k in range(TOP):
        hit = (ids_ref[:, k : k + 1] == lane_expert) & (lane < E)
        value = jnp.sum(jnp.where(hit, per_expert, 0.0), axis=1, keepdims=True)
        result = result + jnp.where(out_lane == k, value, 0.0)
    groute_out[...] = result[0:T, :].astype(BF16)

    for part in range(2):
        each(1, Y, lambda d, part=part: y_copy(part, d, y, y_peer(d)[1]).wait_send())
    for part in range(3):
        each(1, NP, lambda d, part=part: x_copy(part, d, x_peer(d)[0], me, x_peer(d)[1]).wait_send())
    for stream in range(4):
        n = half if stream in (0, 3) else half - 1
        each(0, n, lambda s, stream=stream: hop(stream, s, True).wait_send())
        each(1, n + 1, lambda k, stream=stream: ring(stream, k).wait_send())
    each(1, Z, lambda d: z_copy(d, d, (w, (z + d) % Z)).wait_send())
    for part in range(2):
        each(1, NP, lambda d, part=part: xb_copy(part, d, x_peer(d)[0], me, x_peer(d)[1]).wait_send())
    each(1, Y, lambda d: yb_copy(d, y_peer(d)[0], y, y_peer(d)[1]).wait_send())
    out_copy.wait()


GRID = {64: (4, 8, 2), 8: (2, 2, 2)}


def body(tokens, grad_out, expert_ids, route_weights, w_gate, w_up, w_down):
    X, Y, C = GRID[lax.axis_size("wide")]
    Z = lax.axis_size("narrow")
    T, F = tokens.shape
    TOP = expert_ids.shape[1]
    D, H = w_gate.shape[1:]
    E = X * Y * C
    CAP = min(T, 2 * T * TOP // E)
    TP = -(-T // 16) * 16
    HP = -(-H // LANES) * LANES
    NP = X * C
    PB = Y * CAP
    SLOTS = NP * PB
    TOKS = Y * TP
    half = Z // 2
    A = F // 2
    cfg = dict(X=X, Y=Y, C=C, Z=Z, T=T, TP=TP, F=F, H=H, HP=HP, E=E, TOP=TOP, CAP=CAP)
    ids = jnp.pad(expert_ids, ((0, TP - T), (0, 0)), constant_values=-1)
    gains = jnp.pad(route_weights.astype(F32), ((0, TP - T), (0, 0)))
    vmem = pl.BlockSpec(memory_space=pltpu.VMEM)
    hbm = pl.BlockSpec(memory_space=pl.ANY)
    dma = pltpu.SemaphoreType.DMA
    scratch = [
        pltpu.VMEM((TP, 2 * F + LANES), BF16),
        pltpu.VMEM((TOKS, 2 * F + LANES), BF16),
        pltpu.VMEM((TOKS, SLOTS), BF16),
        pltpu.VMEM((2, SLOTS, LANES), BF16),
        pltpu.VMEM((SLOTS, TOKS), F32),
        pltpu.VMEM((SLOTS, 2 * F + LANES), BF16),
        pltpu.VMEM((Z, SLOTS, F), BF16),
        pltpu.VMEM((Z, SLOTS, F), BF16),
        pltpu.VMEM((SLOTS, LANES), BF16),
        pltpu.VMEM((2 * HP, D), BF16),
        pltpu.VMEM((HP, D), BF16),
        pltpu.VMEM((SLOTS, 2 * HP), F32),
        pltpu.VMEM((SLOTS, HP), F32),
        pltpu.VMEM((SLOTS, 2 * HP), BF16),
        pltpu.VMEM((SLOTS, HP), BF16),
        pltpu.VMEM((4, half + 1, SLOTS, A), BF16),
        pltpu.VMEM((4, half + 1, SLOTS, A), BF16),
        pltpu.VMEM((Z, 8, LANES), F32),
        pltpu.VMEM((8, LANES), F32),
        pltpu.VMEM((8, LANES), F32),
        pltpu.VMEM((NP, 8, LANES), F32),
        pltpu.VMEM((SLOTS, F), BF16),
        pltpu.VMEM((SLOTS, F), BF16),
        pltpu.VMEM((TOKS, F + LANES), BF16),
        pltpu.VMEM((TOKS, F + LANES), BF16),
        pltpu.VMEM((H, D), BF16),
        dma((2, Y)),
        dma((2, Y)),
        dma((3, NP)),
        dma((3, NP)),
        dma((4, half)),
        dma((4, half)),
        dma((4, half + 1)),
        dma((4, half + 1)),
        dma((Z,)),
        dma((Z,)),
        dma((2, NP)),
        dma((2, NP)),
        dma((Y,)),
        dma((Y,)),
        dma((3,)),
        dma,
    ]
    grad_tokens, grad_route, grad_down = pl.pallas_call(
        functools.partial(kernel, cfg),
        out_shape=(
            jax.ShapeDtypeStruct((T, F), BF16),
            jax.ShapeDtypeStruct((T, TOP), BF16),
            jax.ShapeDtypeStruct((H, D), BF16),
        ),
        in_specs=[vmem] * 4 + [hbm] * 3,
        out_specs=(vmem, vmem, hbm),
        scratch_shapes=scratch,
        compiler_params=pltpu.CompilerParams(
            collective_id=0, has_side_effects=True, vmem_limit_bytes=60 * 1024 * 1024
        ),
        name="experts",
    )(ids, gains, tokens, grad_out, w_gate[0].T, w_up[0].T, w_down[0])
    return grad_tokens, grad_route, grad_down[None]


def solution(mesh):
    in_specs = (
        P("wide", "narrow"),
        P("wide", "narrow"),
        P("wide", None),
        P("wide", None),
        P("wide", None, "narrow"),
        P("wide", None, "narrow"),
        P("wide", "narrow", None),
    )
    out_specs = (P("wide", "narrow"), P("wide", None), P("wide", "narrow", None))
    return jax.shard_map(body, mesh=mesh, in_specs=in_specs, out_specs=out_specs, check_vma=False)
```

```python
import functools

import jax
import jax.numpy as jnp
from jax import lax
from jax.experimental import pallas as pl
from jax.experimental.pallas import tpu as pltpu
from jax.sharding import PartitionSpec as P

MESH = pl.DeviceIdType.MESH
F32 = jnp.float32
BF16 = jnp.bfloat16
LANES = 128


def dot_nn(a, b):
    return lax.dot_general(a, b, (((1,), (0,)), ((), ())), preferred_element_type=F32)


def dot_nt(a, b):
    return lax.dot_general(a, b, (((1,), (1,)), ((), ())), preferred_element_type=F32)


def dot_tn(a, b):
    return lax.dot_general(a, b, (((0,), (0,)), ((), ())), preferred_element_type=F32)


def steps_of(value, width, count):
    out = jnp.zeros_like(value)
    for m in range(1, count):
        out = out + (value >= width * m).astype(jnp.int32)
    return out


def kernel(
    cfg,
    ids_ref,
    rw_ref,
    tok_ref,
    grd_ref,
    wg_ref,
    wu_ref,
    wd_ref,
    gtok_out,
    groute_out,
    gdown_out,
    pack,
    ycol,
    place_s,
    place_t,
    emat,
    slot_key,
    sel,
    gtok,
    graw,
    gycol,
    gsel,
    ggrd,
    gain,
    wgu,
    wdn,
    acc_gu,
    acc_bp,
    dcat,
    hidden,
    rs_send,
    rs_recv,
    zroute,
    zroute_own,
    rsum,
    xroute,
    cgrad,
    xback,
    yback_send,
    yback,
    gdown,
    y_snd,
    y_rcv,
    x_snd,
    x_rcv,
    zg_snd,
    zg_rcv,
    yg_snd,
    yg_rcv,
    xg_snd,
    xg_rcv,
    g_snd,
    g_rcv,
    r_snd,
    r_rcv,
    z_snd,
    z_rcv,
    xb_snd,
    xb_rcv,
    yb_snd,
    yb_rcv,
    w_sem,
    o_sem,
):
    X, Y, C, Z = cfg["X"], cfg["Y"], cfg["C"], cfg["Z"]
    T, TP, F, H, HP, E, TOP, CAP = (
        cfg[k] for k in ("T", "TP", "F", "H", "HP", "E", "TOP", "CAP")
    )
    NP = X * C
    PB = Y * CAP
    SLOTS = NP * PB
    TOKS = Y * TP
    half = Z // 2
    A = F // 2

    w = lax.axis_index("wide")
    z = lax.axis_index("narrow")
    x = w // (Y * C)
    y = (w // C) % Y
    c = w % C
    me = x * C + c

    def y_peer(d):
        yy = (y + d) % Y
        return yy, (x * (Y * C) + yy * C + c, z)

    def x_peer(d):
        p = (me + d) % NP
        return p, ((p // C) * (Y * C) + y * C + p % C, z)

    right = (w, (z + 1) % Z)
    left = (w, (z + Z - 1) % Z)

    def rows(block, size):
        return pl.ds(pl.multiple_of(block * size, 16), size)

    def cols(block):
        return pl.ds(pl.multiple_of(block * F, LANES), F)

    def remote(src, dst, snd, rcv, device):
        return pltpu.make_async_remote_copy(
            src_ref=src, dst_ref=dst, send_sem=snd, recv_sem=rcv, device_id=device, device_id_type=MESH
        )

    def each(first, last, body):
        lax.fori_loop(first, last, lambda i, carry: (body(i), carry)[1], 0)

    weights = [
        pltpu.make_async_copy(wg_ref, wgu.at[pl.ds(0, H), :], w_sem.at[0]),
        pltpu.make_async_copy(wu_ref, wgu.at[pl.ds(HP, H), :], w_sem.at[1]),
        pltpu.make_async_copy(wd_ref, wdn.at[pl.ds(0, H), :], w_sem.at[2]),
    ]
    for copy in weights:
        copy.start()

    barrier = pltpu.get_barrier_semaphore()

    def greet(device):
        pl.semaphore_signal(barrier, inc=1, device_id=device, device_id_type=MESH)

    each(1, Y, lambda d: greet(y_peer(d)[1]))
    each(1, NP, lambda d: greet(x_peer(d)[1]))
    each(1, Z, lambda d: greet((w, (z + d) % Z)))

    lane = lax.broadcasted_iota(jnp.int32, (TP, LANES), 1)
    lane_expert = jnp.where(lane >= E, lane - E, lane)
    named = jnp.zeros((TP, LANES), F32)
    weight = jnp.zeros((TP, LANES), F32)
    for k in range(TOP):
        hit = ids_ref[:, k : k + 1] == lane_expert
        named = named + jnp.where(hit, 1.0, 0.0)
        weight = weight + jnp.where(hit, rw_ref[:, k : k + 1], 0.0)
    tri = (
        lax.broadcasted_iota(jnp.int32, (TP, TP), 0) > lax.broadcasted_iota(jnp.int32, (TP, TP), 1)
    ).astype(F32)
    before = dot_nn(tri.astype(BF16), named.astype(BF16))
    table = jnp.where(lane < E, named * (before + 1.0), jnp.where(lane < 2 * E, weight, 0.0))

    pack[...] = jnp.zeros_like(pack)
    pack[0:T, 0:F] = tok_ref[...]
    pack[:, F:] = table.astype(BF16)
    graw[z, 0:T, :] = grd_ref[...]
    graw[:, T:, :] = jnp.zeros((Z, TP - T, F), BF16)

    pl.semaphore_wait(barrier, (Y - 1) + (NP - 1) + (Z - 1))

    def y_copy(d, owner, device):
        return remote(pack, ycol.at[rows(owner, TP), :], y_snd.at[d], y_rcv.at[d], device)

    each(1, Y, lambda d: y_copy(d, y, y_peer(d)[1]).start())

    def zg_copy(d, owner, device):
        here = graw.at[owner, pl.ds(0, T), :]
        return remote(here, here, zg_snd.at[d], zg_rcv.at[d], device)

    def yg_copy(chunk, d, owner, device):
        return remote(
            graw.at[chunk, pl.ds(0, T), :],
            gycol.at[chunk, pl.ds(pl.multiple_of(owner * TP, 16), T), :],
            yg_snd.at[chunk, d],
            yg_rcv.at[chunk, d],
            device,
        )

    def xg_copy(chunk, d, src, dst, device):
        return remote(
            gsel.at[chunk, rows(src, PB), :],
            ggrd.at[chunk, rows(dst, PB), :],
            xg_snd.at[chunk, d],
            xg_rcv.at[chunk, d],
            device,
        )

    each(1, Z, lambda d: zg_copy(d, z, (w, (z + d) % Z)).start())

    def spread_y(chunk):
        each(1, Y, lambda d: yg_copy(chunk, d, y, y_peer(d)[1]).start())
        gycol[chunk, rows(y, TP), :] = graw[chunk]

    def arrive_z(chunk):
        d = (z + Z - chunk) % Z
        zg_copy(d, chunk, (w, (z + d) % Z)).wait_recv()

    def pair(s, act):
        act((z + s) % Z)

        @pl.when(s < half)
        def _():
            act((z + Z - s) % Z)

    def stage_a(s):
        def act(chunk):
            arrive_z(chunk)
            spread_y(chunk)

        pair(s, act)

    def select(chunk):
        def one(d):
            yy = (y + Y - d) % Y
            yg_copy(chunk, d, yy, y_peer(d)[1]).wait_recv()

        each(1, Y, one)
        gsel[chunk] = dot_nn(place_s[...], gycol[chunk]).astype(BF16)

        def send(d):
            p, device = x_peer(d)
            xg_copy(chunk, d, p, me, device).start()

        each(1, NP, send)
        ggrd[chunk, rows(me, PB), :] = gsel[chunk, rows(me, PB), :]

    def arrive_x(chunk):
        def one(d):
            p = (me + NP - d) % NP
            xg_copy(chunk, d, p, p, x_peer(d)[1]).wait_recv()

        each(1, NP, one)
        acc_bp[...] += dot_nt(ggrd[chunk], wdn[:, cols(chunk)])

    spread_y(z)
    ycol[rows(y, TP), :] = pack[...]
    for j in range(Y):
        gycol[:, j * TP + T : (j + 1) * TP, :] = jnp.zeros((Z, TP - T, F), BF16)

    slot = lax.broadcasted_iota(jnp.int32, (SLOTS, LANES), 0)
    slot_lane = lax.broadcasted_iota(jnp.int32, (SLOTS, LANES), 1)
    peer = steps_of(slot, PB, NP)
    peer_x = steps_of(peer, C, X)
    expert = peer_x * (Y * C) + y * C + (peer - peer_x * C)
    emat[0] = (slot_lane == expert).astype(F32).astype(BF16)
    emat[1] = (slot_lane == expert + E).astype(F32).astype(BF16)
    slot = lax.broadcasted_iota(jnp.int32, (SLOTS, TOKS), 0)
    tok_y = steps_of(lax.broadcasted_iota(jnp.int32, (SLOTS, TOKS), 1), TP, Y)
    inner = slot - PB * steps_of(slot, PB, NP)
    slot_y = steps_of(inner, CAP, Y)
    slot_key[...] = jnp.where(tok_y == slot_y, inner - CAP * slot_y + 1, -1).astype(F32)

    wgu[H:HP, :] = jnp.zeros((HP - H, wgu.shape[1]), BF16)
    wgu[HP + H :, :] = jnp.zeros((HP - H, wgu.shape[1]), BF16)
    wdn[H:, :] = jnp.zeros((HP - H, wdn.shape[1]), BF16)

    each(1, Y, lambda d: y_copy(d, (y + Y - d) % Y, y_peer(d)[1]).wait_recv())
    tables = ycol[:, F:]
    place = dot_nt(emat[0], tables) == slot_key[...]
    place_b = place.astype(F32).astype(BF16)
    sel[:, 0:F] = dot_nn(place_b, ycol[:, 0:F]).astype(BF16)

    def x_copy(part, d, src, dst, device):
        if part == 0:
            return remote(
                sel.at[rows(src, PB), pl.ds(0, F)],
                gtok.at[z, rows(dst, PB), :],
                x_snd.at[0, d],
                x_rcv.at[0, d],
                device,
            )
        return remote(
            sel.at[rows(src, PB), pl.ds(F, LANES)],
            gain.at[rows(dst, PB), :],
            x_snd.at[1, d],
            x_rcv.at[1, d],
            device,
        )

    def x_start(part):
        def one(d):
            p, device = x_peer(d)
            x_copy(part, d, p, me, device).start()

        each(1, NP, one)

    def x_wait(part):
        def one(d):
            p = (me + NP - d) % NP
            x_copy(part, d, p, p, x_peer(d)[1]).wait_recv()

        each(1, NP, one)

    x_start(0)
    gtok[z, rows(me, PB), :] = sel[rows(me, PB), 0:F]
    place_s[...] = place_b
    weights_of = jnp.where(place, dot_nt(emat[1], tables), 0.0)
    sel[:, F:] = jnp.broadcast_to(
        jnp.sum(weights_of, axis=1, keepdims=True), (SLOTS, LANES)
    ).astype(BF16)
    x_start(1)
    gain[rows(me, PB), :] = sel[rows(me, PB), F:]
    acc_gu[...] = jnp.zeros_like(acc_gu)
    acc_bp[...] = jnp.zeros_like(acc_bp)
    stage_a(1)

    def hop(stream, s, sending):
        to_right = stream % 2 == 0
        back = s if sending else s + 1
        owner = (z + Z - back) % Z if to_right else (z + back) % Z
        block = gtok.at[owner, pl.ds((stream // 2) * (SLOTS // 2), SLOTS // 2), :]
        return remote(block, block, g_snd.at[stream, s], g_rcv.at[stream, s], right if to_right else left)

    def use_tokens(owner):
        acc_gu[...] += dot_nt(gtok[owner], wgu[:, cols(owner)])

    x_wait(0)
    for stream in range(4):
        hop(stream, 0, True).start()
    select(z)
    stage_a(2)
    for copy in weights:
        copy.wait()
    use_tokens(z)

    key_slot = lax.broadcasted_iota(jnp.int32, (TOKS, SLOTS), 1)
    key_inner = key_slot - PB * steps_of(key_slot, PB, NP)
    key_y = steps_of(key_inner, CAP, Y)
    key_tok = steps_of(lax.broadcasted_iota(jnp.int32, (TOKS, SLOTS), 0), TP, Y)
    key = jnp.where(key_tok == key_y, key_inner - CAP * key_y + 1, -1).astype(F32)
    place_t[...] = (dot_nt(ycol[:, F:], emat[0]) == key).astype(F32).astype(BF16)
    x_wait(1)

    def forward(stream, s):
        hop(stream, s - 1, False).wait_recv()
        if stream in (0, 3):
            hop(stream, s, True).start()
        else:

            @pl.when(s < half - 1)
            def _():
                hop(stream, s, True).start()

    def gather_step(s):
        forward(0, s)
        forward(1, s)

        @pl.when(s < half - 1)
        def _():
            stage_a(s + 2)

        select((z + s) % Z)
        forward(2, s)
        forward(3, s)
        select((z + Z - s) % Z)
        use_tokens((z + Z - s) % Z)
        use_tokens((z + s) % Z)

        @pl.when(s > 2)
        def _():
            pair(s - 2, arrive_x)

    each(1, half, gather_step)
    select((z + half) % Z)
    hop(0, half - 1, False).wait_recv()
    hop(3, half - 1, False).wait_recv()
    use_tokens((z + half) % Z)

    arrive_x(z)
    for s in (half - 2, half - 1, half):
        pair(s, arrive_x)

    gate = acc_gu[:, 0:HP]
    up = acc_gu[:, HP:]
    back = acc_bp[...]
    scale = gain[...].astype(F32)
    sig = jax.nn.sigmoid(gate)
    active = gate * sig
    slope = sig * (1.0 + gate * (1.0 - sig))
    hid = (active * up).astype(BF16)
    hidden[...] = hid
    d_hidden = scale * back
    dcat[:, 0:HP] = (d_hidden * up * slope).astype(BF16)
    dcat[:, HP:] = (d_hidden * active).astype(BF16)
    route = jnp.sum(hid.astype(F32) * back, axis=1, keepdims=True)

    def ring(stream, k):
        return remote(
            rs_send.at[stream, k],
            rs_recv.at[stream, k],
            r_snd.at[stream, k],
            r_rcv.at[stream, k],
            right if stream < 2 else left,
        )

    def partial(owner):
        return dot_nn(dcat[...], wgu[:, cols(owner)])

    def push(stream, k, value, add):
        if add:
            ring(stream, k + 1).wait_recv()
            value = value + rs_recv[stream, k + 1].astype(F32)
        rs_send[stream, k] = value.astype(BF16)
        ring(stream, k).start()

    def down(chunk):
        scaled = (jnp.concatenate([scale_ref()] * (F // LANES), axis=1) * ggrd[chunk].astype(F32)).astype(BF16)
        gdown[:, cols(chunk)] = dot_tn(hidden[...], scaled)[0:H, :].astype(BF16)

    def scale_ref():
        return gain[...].astype(F32)

    far = partial((z + half) % Z)
    push(0, half, far[:, 0:A], False)
    push(3, half, far[:, A:], False)
    to_right = partial((z + half - 1) % Z)
    to_left = partial((z + Z - half + 1) % Z)
    push(1, half - 1, to_right[:, A:], False)
    push(2, half - 1, to_left[:, 0:A], False)

    rt_row = lax.broadcasted_iota(jnp.int32, (SLOTS, LANES), 0)
    rt_inner = rt_row - PB * steps_of(rt_row, PB, NP)
    rt_lane = lax.broadcasted_iota(jnp.int32, (SLOTS, LANES), 1)
    spread = jnp.where(rt_lane == rt_inner, route.astype(BF16).astype(F32), 0.0).astype(BF16)
    blk = lax.broadcasted_iota(jnp.int32, (8, SLOTS), 0)
    blk_of = steps_of(lax.broadcasted_iota(jnp.int32, (8, SLOTS), 1), PB, NP)
    pick = (blk == blk_of).astype(F32).astype(BF16)
    zroute_own[...] = dot_nn(pick, spread)

    def z_copy(d, slot_d, device):
        return remote(zroute_own, zroute.at[slot_d], z_snd.at[d], z_rcv.at[d], device)

    each(1, Z, lambda d: z_copy(d, d, (w, (z + d) % Z)).start())

    push(0, half - 1, to_right[:, 0:A], True)
    push(3, half - 1, to_left[:, A:], True)
    for chunk in range(2):
        down(chunk)

    def reduce_step(i):
        k = half - 1 - i
        to_right = partial((z + k) % Z)
        to_left = partial((z + Z - k) % Z)
        push(0, k, to_right[:, 0:A], True)
        push(3, k, to_left[:, A:], True)
        push(1, k, to_right[:, A:], True)
        push(2, k, to_left[:, 0:A], True)
        per = -(-(Z - 2) // (half - 2))
        for j in range(per):
            chunk = 2 + (i - 1) * per + j

            @pl.when(chunk < Z)
            def _():
                down(chunk)

    each(1, half - 1, reduce_step)
    out_copy = pltpu.make_async_copy(gdown, gdown_out, o_sem)
    out_copy.start()

    each(1, Z, lambda d: z_copy(d, d, (w, (z + d) % Z)).wait_recv())
    total = zroute_own[...]
    for d in range(1, Z):
        total = total + zroute[d]
    rsum[...] = total.astype(BF16).astype(F32)

    def xb_copy(part, d, src, dst, device):
        if part == 0:
            return remote(rsum, xroute.at[dst], xb_snd.at[0, d], xb_rcv.at[0, d], device)
        return remote(
            cgrad.at[rows(src, PB), :],
            xback.at[rows(dst, PB), :],
            xb_snd.at[1, d],
            xb_rcv.at[1, d],
            device,
        )

    def xb_start(part):
        def one(d):
            p, device = x_peer(d)
            xb_copy(part, d, p, me, device).start()

        each(1, NP, one)

    def xb_wait(part):
        def one(d):
            p = (me + NP - d) % NP
            xb_copy(part, d, p, p, x_peer(d)[1]).wait_recv()

        each(1, NP, one)

    xb_start(0)
    xroute[me] = rsum[...]

    own = partial(z)
    for lanes, streams in ((slice(0, A), (0, 2)), (slice(A, F), (1, 3))):
        value = own[:, lanes]
        for stream in streams:
            ring(stream, 1).wait_recv()
            value = value + rs_recv[stream, 1].astype(F32)
        cgrad[:, lanes] = value.astype(BF16)
    xb_start(1)
    xback[rows(me, PB), :] = cgrad[rows(me, PB), :]

    xb_wait(0)
    sub = lax.broadcasted_iota(jnp.int32, (NP, 8, LANES), 1)
    mine = jnp.sum(jnp.where(sub == me, xroute[...], 0.0), axis=1).astype(BF16)
    lane_in = lax.broadcasted_iota(jnp.int32, (LANES, SLOTS), 0)
    slot_in = lax.broadcasted_iota(jnp.int32, (LANES, SLOTS), 1)
    slot_in = slot_in - PB * steps_of(slot_in, PB, NP)
    wide_rows = dot_nn(mine, (lane_in == slot_in).astype(F32).astype(BF16))
    from_peer = lax.broadcasted_iota(jnp.int32, (NP, SLOTS), 0)
    slot_peer = steps_of(lax.broadcasted_iota(jnp.int32, (NP, SLOTS), 1), PB, NP)
    values = jnp.sum(jnp.where(from_peer == slot_peer, wide_rows, 0.0), axis=0, keepdims=True)
    routed = (place_t[...].astype(F32) * values).astype(BF16)
    yback_send[:, F:] = dot_nn(routed, emat[0]).astype(BF16)

    xb_wait(1)
    yback_send[:, 0:F] = dot_nn(place_t[...], xback[...]).astype(BF16)

    def yb_copy(d, src, dst, device):
        return remote(
            yback_send.at[rows(src, TP), :], yback.at[rows(dst, TP), :], yb_snd.at[d], yb_rcv.at[d], device
        )

    def yb_start(d):
        yy, device = y_peer(d)
        yb_copy(d, yy, y, device).start()

    each(1, Y, yb_start)
    yback[rows(y, TP), :] = yback_send[rows(y, TP), :]

    def yb_wait(d):
        yy = (y + Y - d) % Y
        yb_copy(d, yy, yy, y_peer(d)[1]).wait_recv()

    each(1, Y, yb_wait)
    final = jnp.zeros((TP, F + LANES), F32)
    for j in range(Y):
        final = final + yback[j * TP : (j + 1) * TP, :].astype(F32)
    gtok_out[...] = final[0:T, 0:F].astype(BF16)
    per_expert = final[:, F:]
    out_lane = lax.broadcasted_iota(jnp.int32, (TP, TOP), 1)
    result = jnp.zeros((TP, TOP), F32)
    for k in range(TOP):
        hit = (ids_ref[:, k : k + 1] == lane_expert) & (lane < E)
        value = jnp.sum(jnp.where(hit, per_expert, 0.0), axis=1, keepdims=True)
        result = result + jnp.where(out_lane == k, value, 0.0)
    groute_out[...] = result[0:T, :].astype(BF16)

    each(1, Y, lambda d: y_copy(d, y, y_peer(d)[1]).wait_send())
    for part in range(2):
        each(1, NP, lambda d, part=part: x_copy(part, d, x_peer(d)[0], me, x_peer(d)[1]).wait_send())
    each(1, Z, lambda d: zg_copy(d, z, (w, (z + d) % Z)).wait_send())

    def chunk_sent(chunk):
        each(1, Y, lambda d: yg_copy(chunk, d, y, y_peer(d)[1]).wait_send())
        each(1, NP, lambda d: xg_copy(chunk, d, x_peer(d)[0], me, x_peer(d)[1]).wait_send())

    each(0, Z, chunk_sent)
    for stream in range(4):
        n = half if stream in (0, 3) else half - 1
        each(0, n, lambda s, stream=stream: hop(stream, s, True).wait_send())
        each(1, n + 1, lambda k, stream=stream: ring(stream, k).wait_send())
    each(1, Z, lambda d: z_copy(d, d, (w, (z + d) % Z)).wait_send())
    for part in range(2):
        each(1, NP, lambda d, part=part: xb_copy(part, d, x_peer(d)[0], me, x_peer(d)[1]).wait_send())
    each(1, Y, lambda d: yb_copy(d, y_peer(d)[0], y, y_peer(d)[1]).wait_send())
    out_copy.wait()


GRID = {64: (4, 8, 2), 8: (2, 2, 2)}


def body(tokens, grad_out, expert_ids, route_weights, w_gate, w_up, w_down):
    X, Y, C = GRID[lax.axis_size("wide")]
    Z = lax.axis_size("narrow")
    T, F = tokens.shape
    TOP = expert_ids.shape[1]
    D, H = w_gate.shape[1:]
    E = X * Y * C
    CAP = min(T, 2 * T * TOP // E)
    TP = -(-T // 16) * 16
    HP = -(-H // LANES) * LANES
    NP = X * C
    PB = Y * CAP
    SLOTS = NP * PB
    TOKS = Y * TP
    half = Z // 2
    A = F // 2
    cfg = dict(X=X, Y=Y, C=C, Z=Z, T=T, TP=TP, F=F, H=H, HP=HP, E=E, TOP=TOP, CAP=CAP)
    ids = jnp.pad(expert_ids, ((0, TP - T), (0, 0)), constant_values=-1)
    gains = jnp.pad(route_weights.astype(F32), ((0, TP - T), (0, 0)))
    vmem = pl.BlockSpec(memory_space=pltpu.VMEM)
    hbm = pl.BlockSpec(memory_space=pl.ANY)
    dma = pltpu.SemaphoreType.DMA
    scratch = [
        pltpu.VMEM((TP, F + LANES), BF16),
        pltpu.VMEM((TOKS, F + LANES), BF16),
        pltpu.VMEM((SLOTS, TOKS), BF16),
        pltpu.VMEM((TOKS, SLOTS), BF16),
        pltpu.VMEM((2, SLOTS, LANES), BF16),
        pltpu.VMEM((SLOTS, TOKS), F32),
        pltpu.VMEM((SLOTS, F + LANES), BF16),
        pltpu.VMEM((Z, SLOTS, F), BF16),
        pltpu.VMEM((Z, TP, F), BF16),
        pltpu.VMEM((Z, TOKS, F), BF16),
        pltpu.VMEM((Z, SLOTS, F), BF16),
        pltpu.VMEM((Z, SLOTS, F), BF16),
        pltpu.VMEM((SLOTS, LANES), BF16),
        pltpu.VMEM((2 * HP, D), BF16),
        pltpu.VMEM((HP, D), BF16),
        pltpu.VMEM((SLOTS, 2 * HP), F32),
        pltpu.VMEM((SLOTS, HP), F32),
        pltpu.VMEM((SLOTS, 2 * HP), BF16),
        pltpu.VMEM((SLOTS, HP), BF16),
        pltpu.VMEM((4, half + 1, SLOTS, A), BF16),
        pltpu.VMEM((4, half + 1, SLOTS, A), BF16),
        pltpu.VMEM((Z, 8, LANES), F32),
        pltpu.VMEM((8, LANES), F32),
        pltpu.VMEM((8, LANES), F32),
        pltpu.VMEM((NP, 8, LANES), F32),
        pltpu.VMEM((SLOTS, F), BF16),
        pltpu.VMEM((SLOTS, F), BF16),
        pltpu.VMEM((TOKS, F + LANES), BF16),
        pltpu.VMEM((TOKS, F + LANES), BF16),
        pltpu.VMEM((H, D), BF16),
        dma((Y,)),
        dma((Y,)),
        dma((2, NP)),
        dma((2, NP)),
        dma((Z,)),
        dma((Z,)),
        dma((Z, Y)),
        dma((Z, Y)),
        dma((Z, NP)),
        dma((Z, NP)),
        dma((4, half)),
        dma((4, half)),
        dma((4, half + 1)),
        dma((4, half + 1)),
        dma((Z,)),
        dma((Z,)),
        dma((2, NP)),
        dma((2, NP)),
        dma((Y,)),
        dma((Y,)),
        dma((3,)),
        dma,
    ]
    grad_tokens, grad_route, grad_down = pl.pallas_call(
        functools.partial(kernel, cfg),
        out_shape=(
            jax.ShapeDtypeStruct((T, F), BF16),
            jax.ShapeDtypeStruct((T, TOP), BF16),
            jax.ShapeDtypeStruct((H, D), BF16),
        ),
        in_specs=[vmem] * 4 + [hbm] * 3,
        out_specs=(vmem, vmem, hbm),
        scratch_shapes=scratch,
        compiler_params=pltpu.CompilerParams(
            collective_id=0, has_side_effects=True, vmem_limit_bytes=60 * 1024 * 1024
        ),
        name="experts",
    )(ids, gains, tokens, grad_out, w_gate[0].T, w_up[0].T, w_down[0])
    return grad_tokens, grad_route, grad_down[None]


def solution(mesh):
    in_specs = (
        P("wide", "narrow"),
        P("wide", "narrow"),
        P("wide", None),
        P("wide", None),
        P("wide", None, "narrow"),
        P("wide", None, "narrow"),
        P("wide", "narrow", None),
    )
    out_specs = (P("wide", "narrow"), P("wide", None), P("wide", "narrow", None))
    return jax.shard_map(body, mesh=mesh, in_specs=in_specs, out_specs=out_specs, check_vma=False)
```

```python
import functools

import jax
import jax.numpy as jnp
from jax import lax
from jax.experimental import pallas as pl
from jax.experimental.pallas import tpu as pltpu
from jax.sharding import PartitionSpec as P

MESH = pl.DeviceIdType.MESH
F32 = jnp.float32
BF16 = jnp.bfloat16
LANES = 128


def dot_nn(a, b):
    return lax.dot_general(a, b, (((1,), (0,)), ((), ())), preferred_element_type=F32)


def dot_nt(a, b):
    return lax.dot_general(a, b, (((1,), (1,)), ((), ())), preferred_element_type=F32)


def dot_tn(a, b):
    return lax.dot_general(a, b, (((0,), (0,)), ((), ())), preferred_element_type=F32)


def steps_of(value, width, count):
    out = jnp.zeros_like(value)
    for m in range(1, count):
        out = out + (value >= width * m).astype(jnp.int32)
    return out


def kernel(
    cfg,
    ids_ref,
    rw_ref,
    tok_ref,
    grd_ref,
    wg_ref,
    wu_ref,
    wd_ref,
    gtok_out,
    groute_out,
    gdown_out,
    pack,
    ycol,
    place_s,
    place_t,
    emat,
    slot_key,
    sel,
    gtok,
    graw,
    gycol,
    gsel,
    ggrd,
    gain,
    wgu,
    wdn,
    acc_gu,
    acc_bp,
    dcat,
    hidden_t,
    rs_send,
    rs_recv,
    bsend,
    bslot,
    btok,
    bcol,
    bsum,
    bown,
    bdone,
    zroute,
    zroute_own,
    rsum,
    xroute,
    cgrad,
    xback,
    yback_send,
    yback,
    gdown,
    y_snd,
    y_rcv,
    x_snd,
    x_rcv,
    zg_snd,
    zg_rcv,
    yg_snd,
    yg_rcv,
    xg_snd,
    xg_rcv,
    g_snd,
    g_rcv,
    r_snd,
    r_rcv,
    z_snd,
    z_rcv,
    xp_snd,
    xp_rcv,
    yp_snd,
    yp_rcv,
    zp_snd,
    zp_rcv,
    xb_snd,
    xb_rcv,
    yb_snd,
    yb_rcv,
    w_sem,
    o_sem,
):
    X, Y, C, Z = cfg["X"], cfg["Y"], cfg["C"], cfg["Z"]
    T, TP, F, H, HP, E, TOP, CAP = (
        cfg[k] for k in ("T", "TP", "F", "H", "HP", "E", "TOP", "CAP")
    )
    NP = X * C
    PB = Y * CAP
    SLOTS = NP * PB
    TOKS = Y * TP
    half = Z // 2
    A = F // 2

    w = lax.axis_index("wide")
    z = lax.axis_index("narrow")
    x = w // (Y * C)
    y = (w // C) % Y
    c = w % C
    me = x * C + c

    def y_peer(d):
        yy = (y + d) % Y
        return yy, (x * (Y * C) + yy * C + c, z)

    def x_peer(d):
        p = (me + d) % NP
        return p, ((p // C) * (Y * C) + y * C + p % C, z)

    right = (w, (z + 1) % Z)
    left = (w, (z + Z - 1) % Z)

    def rows(block, size):
        return pl.ds(pl.multiple_of(block * size, 16), size)

    def cols(block):
        return pl.ds(pl.multiple_of(block * F, LANES), F)

    def remote(src, dst, snd, rcv, device):
        return pltpu.make_async_remote_copy(
            src_ref=src, dst_ref=dst, send_sem=snd, recv_sem=rcv, device_id=device, device_id_type=MESH
        )

    def each(first, last, body):
        lax.fori_loop(first, last, lambda i, carry: (body(i), carry)[1], 0)

    weights = [
        pltpu.make_async_copy(wg_ref, wgu.at[pl.ds(0, H), :], w_sem.at[0]),
        pltpu.make_async_copy(wu_ref, wgu.at[pl.ds(HP, H), :], w_sem.at[1]),
        pltpu.make_async_copy(wd_ref, wdn.at[pl.ds(0, H), :], w_sem.at[2]),
    ]
    for copy in weights:
        copy.start()

    barrier = pltpu.get_barrier_semaphore()

    def greet(device):
        pl.semaphore_signal(barrier, inc=1, device_id=device, device_id_type=MESH)

    each(1, Y, lambda d: greet(y_peer(d)[1]))
    each(1, NP, lambda d: greet(x_peer(d)[1]))
    each(1, Z, lambda d: greet((w, (z + d) % Z)))

    lane = lax.broadcasted_iota(jnp.int32, (TP, LANES), 1)
    lane_expert = jnp.where(lane >= E, lane - E, lane)
    named = jnp.zeros((TP, LANES), F32)
    weight = jnp.zeros((TP, LANES), F32)
    for k in range(TOP):
        hit = ids_ref[:, k : k + 1] == lane_expert
        named = named + jnp.where(hit, 1.0, 0.0)
        weight = weight + jnp.where(hit, rw_ref[:, k : k + 1], 0.0)
    tri = (
        lax.broadcasted_iota(jnp.int32, (TP, TP), 0) > lax.broadcasted_iota(jnp.int32, (TP, TP), 1)
    ).astype(F32)
    before = dot_nn(tri.astype(BF16), named.astype(BF16))
    table = jnp.where(lane < E, named * (before + 1.0), jnp.where(lane < 2 * E, weight, 0.0))

    pack[...] = jnp.zeros_like(pack)
    pack[0:T, 0:F] = tok_ref[...]
    pack[:, F:] = table.astype(BF16)
    graw[0, 0:T, 0:F] = grd_ref[...]

    pl.semaphore_wait(barrier, (Y - 1) + (NP - 1) + (Z - 1))

    def y_copy(d, owner, device):
        return remote(pack, ycol.at[rows(owner, TP), :], y_snd.at[d], y_rcv.at[d], device)

    each(1, Y, lambda d: y_copy(d, y, y_peer(d)[1]).start())

    def first(s):
        return (z + s) % Z

    def second(s):
        return (z + Z - s + half * (1 - jnp.minimum(s, 1))) % Z

    def zg_copy(d, s, part):
        return remote(
            graw.at[0, pl.ds(0, T), pl.ds(0, F)],
            graw.at[s, pl.ds(0, T), pl.ds(part * F, F)],
            zg_snd.at[d],
            zg_rcv.at[d],
            (w, (z + d) % Z),
        )

    def yg_copy(s, d, owner, device):
        return remote(
            graw.at[s, pl.ds(0, T), :],
            gycol.at[s, pl.ds(pl.multiple_of(owner * TP, 16), T), :],
            yg_snd.at[s, d],
            yg_rcv.at[s, d],
            device,
        )

    def xg_copy(s, d, src, dst, device):
        return remote(
            gsel.at[s, rows(src, PB), :],
            ggrd.at[s, rows(dst, PB), :],
            xg_snd.at[s, d],
            xg_rcv.at[s, d],
            device,
        )

    def zg_start(d):
        zg_copy(d, d, 1).start()
        zg_copy(Z - d, d, 0).start()

    each(1, half, zg_start)
    zg_copy(half, 0, 1).start()

    def spread_y(s):
        each(1, Y, lambda d: yg_copy(s, d, y, y_peer(d)[1]).start())
        gycol[s, pl.ds(pl.multiple_of(y * TP, 16), T), :] = graw[s, 0:T, :]

    def stage_a(s):
        zg_copy(s, s, 1).wait_recv()
        zg_copy(Z - s, s, 0).wait_recv()
        spread_y(s)

    def select(s):
        def one(d):
            yy = (y + Y - d) % Y
            yg_copy(s, d, yy, y_peer(d)[1]).wait_recv()

        each(1, Y, one)
        gsel[s] = dot_nn(place_s[...], gycol[s]).astype(BF16)

        def send(d):
            p, device = x_peer(d)
            xg_copy(s, d, p, me, device).start()

        each(1, NP, send)
        ggrd[s, rows(me, PB), :] = gsel[s, rows(me, PB), :]

    def arrive_x(s):
        def one(d):
            p = (me + NP - d) % NP
            xg_copy(s, d, p, p, x_peer(d)[1]).wait_recv()

        each(1, NP, one)
        acc_bp[...] += dot_nt(ggrd[s, :, 0:F], wdn[:, cols(first(s))])
        acc_bp[...] += dot_nt(ggrd[s, :, F:], wdn[:, cols(second(s))])

    ycol[rows(y, TP), :] = pack[...]
    for j in range(Y):
        gycol[:, j * TP + T : (j + 1) * TP, :] = jnp.zeros((half, TP - T, 2 * F), BF16)

    slot = lax.broadcasted_iota(jnp.int32, (SLOTS, LANES), 0)
    slot_lane = lax.broadcasted_iota(jnp.int32, (SLOTS, LANES), 1)
    peer = steps_of(slot, PB, NP)
    peer_x = steps_of(peer, C, X)
    expert = peer_x * (Y * C) + y * C + (peer - peer_x * C)
    emat[0] = (slot_lane == expert).astype(F32).astype(BF16)
    emat[1] = (slot_lane == expert + E).astype(F32).astype(BF16)
    slot = lax.broadcasted_iota(jnp.int32, (SLOTS, TOKS), 0)
    tok_y = steps_of(lax.broadcasted_iota(jnp.int32, (SLOTS, TOKS), 1), TP, Y)
    inner = slot - PB * steps_of(slot, PB, NP)
    slot_y = steps_of(inner, CAP, Y)
    slot_key[...] = jnp.where(tok_y == slot_y, inner - CAP * slot_y + 1, -1).astype(F32)

    wgu[H:HP, :] = jnp.zeros((HP - H, wgu.shape[1]), BF16)
    wgu[HP + H :, :] = jnp.zeros((HP - H, wgu.shape[1]), BF16)
    wdn[H:, :] = jnp.zeros((HP - H, wdn.shape[1]), BF16)

    each(1, Y, lambda d: y_copy(d, (y + Y - d) % Y, y_peer(d)[1]).wait_recv())
    tables = ycol[:, F:]
    place = dot_nt(emat[0], tables) == slot_key[...]
    place_b = place.astype(F32).astype(BF16)
    sel[:, 0:F] = dot_nn(place_b, ycol[:, 0:F]).astype(BF16)

    def x_copy(part, d, src, dst, device):
        if part == 0:
            return remote(
                sel.at[rows(src, PB), pl.ds(0, F)],
                gtok.at[z, rows(dst, PB), :],
                x_snd.at[0, d],
                x_rcv.at[0, d],
                device,
            )
        return remote(
            sel.at[rows(src, PB), pl.ds(F, LANES)],
            gain.at[rows(dst, PB), :],
            x_snd.at[1, d],
            x_rcv.at[1, d],
            device,
        )

    def x_start(part):
        def one(d):
            p, device = x_peer(d)
            x_copy(part, d, p, me, device).start()

        each(1, NP, one)

    def x_wait(part):
        def one(d):
            p = (me + NP - d) % NP
            x_copy(part, d, p, p, x_peer(d)[1]).wait_recv()

        each(1, NP, one)

    x_start(0)
    gtok[z, rows(me, PB), :] = sel[rows(me, PB), 0:F]
    place_s[...] = place_b
    weights_of = jnp.where(place, dot_nt(emat[1], tables), 0.0)
    sel[:, F:] = jnp.broadcast_to(
        jnp.sum(weights_of, axis=1, keepdims=True), (SLOTS, LANES)
    ).astype(BF16)
    x_start(1)
    gain[rows(me, PB), :] = sel[rows(me, PB), F:]
    acc_gu[...] = jnp.zeros_like(acc_gu)
    acc_bp[...] = jnp.zeros_like(acc_bp)
    stage_a(1)

    def hop(stream, s, sending):
        to_right = stream % 2 == 0
        back = s if sending else s + 1
        owner = (z + Z - back) % Z if to_right else (z + back) % Z
        block = gtok.at[owner, pl.ds((stream // 2) * (SLOTS // 2), SLOTS // 2), :]
        return remote(block, block, g_snd.at[stream, s], g_rcv.at[stream, s], right if to_right else left)

    def use_tokens(owner):
        acc_gu[...] += dot_nt(gtok[owner], wgu[:, cols(owner)])

    x_wait(0)
    for stream in range(4):
        hop(stream, 0, True).start()
    stage_a(2)
    for copy in weights:
        copy.wait()
    use_tokens(z)
    select(1)

    key_slot = lax.broadcasted_iota(jnp.int32, (TOKS, SLOTS), 1)
    key_inner = key_slot - PB * steps_of(key_slot, PB, NP)
    key_y = steps_of(key_inner, CAP, Y)
    key_tok = steps_of(lax.broadcasted_iota(jnp.int32, (TOKS, SLOTS), 0), TP, Y)
    key = jnp.where(key_tok == key_y, key_inner - CAP * key_y + 1, -1).astype(F32)
    place_t[...] = (dot_nt(ycol[:, F:], emat[0]) == key).astype(F32).astype(BF16)
    x_wait(1)

    def forward(stream, s):
        hop(stream, s - 1, False).wait_recv()
        if stream in (0, 3):
            hop(stream, s, True).start()
        else:

            @pl.when(s < half - 1)
            def _():
                hop(stream, s, True).start()

    def gather_step(s):
        forward(0, s)
        forward(1, s)

        @pl.when(s < half - 2)
        def _():
            stage_a(s + 2)

        @pl.when(s == half - 2)
        def _():
            zg_copy(half, 0, 1).wait_recv()
            spread_y(0)

        forward(2, s)
        forward(3, s)
        select((s + 1) % half)
        use_tokens((z + Z - s) % Z)
        use_tokens((z + s) % Z)

        @pl.when(s > 1)
        def _():
            arrive_x(s - 1)

    each(1, half, gather_step)
    hop(0, half - 1, False).wait_recv()
    hop(3, half - 1, False).wait_recv()
    use_tokens((z + half) % Z)
    arrive_x(half - 1)
    arrive_x(0)

    gate = acc_gu[:, 0:HP]
    up = acc_gu[:, HP:]
    back = acc_bp[...]
    scale = gain[...].astype(F32)
    sig = jax.nn.sigmoid(gate)
    active = gate * sig
    slope = sig * (1.0 + gate * (1.0 - sig))
    hid = (active * up).astype(BF16)
    hidden_t[...] = jnp.transpose(hid.astype(F32)).astype(BF16)
    d_hidden = scale * back
    dcat[:, 0:HP] = (d_hidden * up * slope).astype(BF16)
    dcat[:, HP:] = (d_hidden * active).astype(BF16)
    route = jnp.sum(hid.astype(F32) * back, axis=1, keepdims=True)

    R = SLOTS // 2

    def ring(stream, k):
        return remote(
            rs_send.at[stream, k],
            rs_recv.at[stream, k],
            r_snd.at[stream, k],
            r_rcv.at[stream, k],
            right if stream % 2 == 0 else left,
        )

    def partial(owner, part):
        lanes = pl.ds(pl.multiple_of(owner * F + part * A, LANES), A)
        return dot_nn(dcat[...], wgu[:, lanes])

    def push(stream, k, values, add):
        value = values[(stream // 2) * R : (stream // 2 + 1) * R]
        if add:
            ring(stream, k + 1).wait_recv()
            value = value + rs_recv[stream, k + 1].astype(F32)
        rs_send[stream, k] = value.astype(BF16)
        ring(stream, k).start()

    def down(s, part):
        owner = second(s) if part else first(s)
        scale = gain[...].astype(F32)
        rows_of = ggrd[s, :, part * F : (part + 1) * F].astype(F32)
        scaled = (jnp.concatenate([scale] * (F // LANES), axis=1) * rows_of).astype(BF16)
        gdown[:, cols(owner)] = dot_nn(hidden_t[...], scaled)[0:H, :].astype(BF16)

    def xp_copy(s, d, src, dst, device):
        return remote(
            bsend.at[s, rows(src, PB), :],
            bslot.at[s, rows(dst, PB), :],
            xp_snd.at[s, d],
            xp_rcv.at[s, d],
            device,
        )

    def yp_copy(s, d, src, dst, device):
        return remote(
            btok.at[s, pl.ds(pl.multiple_of(src * TP, 16), T), :],
            bcol.at[s, pl.ds(pl.multiple_of(dst * TP, 16), T), :],
            yp_snd.at[s, d],
            yp_rcv.at[s, d],
            device,
        )

    def zp_copy(s, part, d):
        return remote(
            bsum.at[s, pl.ds(0, T), pl.ds(part * A, A)],
            bdone.at[d, pl.ds(0, T), :],
            zp_snd.at[d],
            zp_rcv.at[d],
            (w, (z + d) % Z),
        )

    def back_x(s):
        bsend[s, :, 0:A] = partial(first(s), 1).astype(BF16)
        bsend[s, :, A:] = partial(second(s), 1).astype(BF16)

        def send(d):
            p, device = x_peer(d)
            xp_copy(s, d, p, me, device).start()

        each(1, NP, send)
        bslot[s, rows(me, PB), :] = bsend[s, rows(me, PB), :]

    def back_y(s):
        def one(d):
            p = (me + NP - d) % NP
            xp_copy(s, d, p, p, x_peer(d)[1]).wait_recv()

        each(1, NP, one)
        btok[s] = dot_nn(place_t[...], bslot[s]).astype(BF16)

        def send(d):
            yy, device = y_peer(d)
            yp_copy(s, d, yy, y, device).start()

        each(1, Y, send)
        here = pl.ds(pl.multiple_of(y * TP, 16), T)
        bcol[s, here, :] = btok[s, here, :]

    def back_z(s):
        def one(d):
            yy = (y + Y - d) % Y
            yp_copy(s, d, yy, yy, y_peer(d)[1]).wait_recv()

        each(1, Y, one)
        total = bcol[s, 0:T, :].astype(F32)
        for j in range(1, Y):
            total = total + bcol[s, j * TP : j * TP + T, :].astype(F32)
        bsum[s, 0:T, :] = total.astype(BF16)
        return total

    def back_z_pair(s):
        back_z(s)
        zp_copy(s, 0, s).start()
        zp_copy(s, 1, Z - s).start()

    far = partial((z + half) % Z, 0)
    push(0, half, far, False)
    push(3, half, far, False)
    back_x(0)
    to_right = partial((z + half - 1) % Z, 0)
    to_left = partial((z + Z - half + 1) % Z, 0)
    push(2, half - 1, to_right, False)
    push(1, half - 1, to_left, False)
    back_x(half - 1)

    rt_row = lax.broadcasted_iota(jnp.int32, (SLOTS, LANES), 0)
    rt_inner = rt_row - PB * steps_of(rt_row, PB, NP)
    rt_lane = lax.broadcasted_iota(jnp.int32, (SLOTS, LANES), 1)
    spread = jnp.where(rt_lane == rt_inner, route.astype(BF16).astype(F32), 0.0).astype(BF16)
    blk = lax.broadcasted_iota(jnp.int32, (8, SLOTS), 0)
    blk_of = steps_of(lax.broadcasted_iota(jnp.int32, (8, SLOTS), 1), PB, NP)
    pick = (blk == blk_of).astype(F32).astype(BF16)
    zroute_own[...] = dot_nn(pick, spread)

    def z_copy(d, slot_d, device):
        return remote(zroute_own, zroute.at[slot_d], z_snd.at[d], z_rcv.at[d], device)

    each(1, Z, lambda d: z_copy(d, d, (w, (z + d) % Z)).start())

    push(0, half - 1, to_right, True)
    push(3, half - 1, to_left, True)

    def reduce_step(k):
        to_right = partial((z + k) % Z, 0)
        to_left = partial((z + Z - k) % Z, 0)
        push(0, k, to_right, True)
        push(1, k, to_left, True)
        push(2, k, to_right, True)
        push(3, k, to_left, True)

    def reduce_loop(i):
        k = half - 1 - i
        reduce_step(k)

        @pl.when(k > 1)
        def _():
            back_x(k - 1)

        back_y((k + 2) % half)

        @pl.when(k < half - 4)
        def _():
            back_z_pair(k + 4)

        down(k, 0)

    back_x(half - 2)
    each(1, half - 1, reduce_loop)
    each(1, Z, lambda d: z_copy(d, d, (w, (z + d) % Z)).wait_recv())
    total = zroute_own[...]
    for d in range(1, Z):
        total = total + zroute[d]
    rsum[...] = total.astype(BF16).astype(F32)

    def xb_copy(part, d, src, dst, device):
        if part == 0:
            return remote(rsum, xroute.at[dst], xb_snd.at[0, d], xb_rcv.at[0, d], device)
        return remote(
            cgrad.at[rows(src, PB), :],
            xback.at[rows(dst, PB), :],
            xb_snd.at[1, d],
            xb_rcv.at[1, d],
            device,
        )

    def xb_start(part):
        def one(d):
            p, device = x_peer(d)
            xb_copy(part, d, p, me, device).start()

        each(1, NP, one)

    def xb_wait(part):
        def one(d):
            p = (me + NP - d) % NP
            xb_copy(part, d, p, p, x_peer(d)[1]).wait_recv()

        each(1, NP, one)

    xb_start(0)
    xroute[me] = rsum[...]

    own = partial(z, 0)
    for part in range(2):
        here = slice(part * R, (part + 1) * R)
        value = own[here]
        for stream in (2 * part, 2 * part + 1):
            ring(stream, 1).wait_recv()
            value = value + rs_recv[stream, 1].astype(F32)
        cgrad[here, :] = value.astype(BF16)
    xb_start(1)
    xback[rows(me, PB), :] = cgrad[rows(me, PB), :]
    back_y(2)
    back_z_pair(4)
    back_y(1)
    bown[...] = back_z(0)[:, 0:A]
    zp_copy(0, 1, half).start()
    back_z_pair(3)

    xb_wait(0)
    sub = lax.broadcasted_iota(jnp.int32, (NP, 8, LANES), 1)
    mine = jnp.sum(jnp.where(sub == me, xroute[...], 0.0), axis=1).astype(BF16)
    lane_in = lax.broadcasted_iota(jnp.int32, (LANES, SLOTS), 0)
    slot_in = lax.broadcasted_iota(jnp.int32, (LANES, SLOTS), 1)
    slot_in = slot_in - PB * steps_of(slot_in, PB, NP)
    wide_rows = dot_nn(mine, (lane_in == slot_in).astype(F32).astype(BF16))
    from_peer = lax.broadcasted_iota(jnp.int32, (NP, SLOTS), 0)
    slot_peer = steps_of(lax.broadcasted_iota(jnp.int32, (NP, SLOTS), 1), PB, NP)
    values = jnp.sum(jnp.where(from_peer == slot_peer, wide_rows, 0.0), axis=0, keepdims=True)
    routed = (place_t[...].astype(F32) * values).astype(BF16)
    yback_send[:, A:] = dot_nn(routed, emat[0]).astype(BF16)

    xb_wait(1)
    yback_send[:, 0:A] = dot_nn(place_t[...], xback[...]).astype(BF16)

    def yb_copy(d, src, dst, device):
        return remote(
            yback_send.at[rows(src, TP), :], yback.at[rows(dst, TP), :], yb_snd.at[d], yb_rcv.at[d], device
        )

    def yb_start(d):
        yy, device = y_peer(d)
        yb_copy(d, yy, y, device).start()

    each(1, Y, yb_start)
    yback[rows(y, TP), :] = yback_send[rows(y, TP), :]
    back_z_pair(2)
    back_z_pair(1)
    each(1, half - 1, lambda s: down(s, 1))
    for s in (0, half - 1):
        down(s, 0)
        down(s, 1)
    out_copy = pltpu.make_async_copy(gdown, gdown_out, o_sem)
    out_copy.start()

    def yb_wait(d):
        yy = (y + Y - d) % Y
        yb_copy(d, yy, yy, y_peer(d)[1]).wait_recv()

    each(1, Y, yb_wait)
    final = jnp.zeros((TP, A + LANES), F32)
    for j in range(Y):
        final = final + yback[j * TP : (j + 1) * TP, :].astype(F32)
    gtok_out[:, 0:A] = final[0:T, 0:A].astype(BF16)
    per_expert = final[:, A:]
    out_lane = lax.broadcasted_iota(jnp.int32, (TP, TOP), 1)
    result = jnp.zeros((TP, TOP), F32)
    for k in range(TOP):
        hit = (ids_ref[:, k : k + 1] == lane_expert) & (lane < E)
        value = jnp.sum(jnp.where(hit, per_expert, 0.0), axis=1, keepdims=True)
        result = result + jnp.where(out_lane == k, value, 0.0)
    groute_out[...] = result[0:T, :].astype(BF16)

    def done(d):
        zp_copy(0, 0, d).wait_recv()

    each(1, Z, done)
    rest = bown[...]
    for d in range(1, Z):
        rest = rest + bdone[d, 0:T, :].astype(F32)
    gtok_out[:, A:] = rest.astype(BF16)

    each(1, Y, lambda d: y_copy(d, y, y_peer(d)[1]).wait_send())
    for part in range(2):
        each(1, NP, lambda d, part=part: x_copy(part, d, x_peer(d)[0], me, x_peer(d)[1]).wait_send())
    each(1, Z, lambda d: zg_copy(d, 0, 1).wait_send())

    def chunk_sent(chunk):
        each(1, Y, lambda d: yg_copy(chunk, d, y, y_peer(d)[1]).wait_send())
        each(1, NP, lambda d: xg_copy(chunk, d, x_peer(d)[0], me, x_peer(d)[1]).wait_send())
        each(1, NP, lambda d: xp_copy(chunk, d, x_peer(d)[0], me, x_peer(d)[1]).wait_send())
        each(1, Y, lambda d: yp_copy(chunk, d, y_peer(d)[0], y, y_peer(d)[1]).wait_send())

    each(0, half, chunk_sent)
    each(1, Z, lambda d: zp_copy(0, 0, d).wait_send())
    for stream in range(4):
        n = half if stream in (0, 3) else half - 1
        each(0, n, lambda s, stream=stream: hop(stream, s, True).wait_send())
        each(1, n + 1, lambda k, stream=stream: ring(stream, k).wait_send())
    each(1, Z, lambda d: z_copy(d, d, (w, (z + d) % Z)).wait_send())
    for part in range(2):
        each(1, NP, lambda d, part=part: xb_copy(part, d, x_peer(d)[0], me, x_peer(d)[1]).wait_send())
    each(1, Y, lambda d: yb_copy(d, y_peer(d)[0], y, y_peer(d)[1]).wait_send())
    out_copy.wait()


GRID = {64: (4, 8, 2), 8: (2, 2, 2)}


def body(tokens, grad_out, expert_ids, route_weights, w_gate, w_up, w_down):
    X, Y, C = GRID[lax.axis_size("wide")]
    Z = lax.axis_size("narrow")
    T, F = tokens.shape
    TOP = expert_ids.shape[1]
    D, H = w_gate.shape[1:]
    E = X * Y * C
    CAP = min(T, 2 * T * TOP // E)
    TP = -(-T // 16) * 16
    HP = -(-H // LANES) * LANES
    NP = X * C
    PB = Y * CAP
    SLOTS = NP * PB
    TOKS = Y * TP
    half = Z // 2
    A = F // 2
    cfg = dict(X=X, Y=Y, C=C, Z=Z, T=T, TP=TP, F=F, H=H, HP=HP, E=E, TOP=TOP, CAP=CAP)
    ids = jnp.pad(expert_ids, ((0, TP - T), (0, 0)), constant_values=-1)
    gains = jnp.pad(route_weights.astype(F32), ((0, TP - T), (0, 0)))
    vmem = pl.BlockSpec(memory_space=pltpu.VMEM)
    hbm = pl.BlockSpec(memory_space=pl.ANY)
    dma = pltpu.SemaphoreType.DMA
    scratch = [
        pltpu.VMEM((TP, F + LANES), BF16),
        pltpu.VMEM((TOKS, F + LANES), BF16),
        pltpu.VMEM((SLOTS, TOKS), BF16),
        pltpu.VMEM((TOKS, SLOTS), BF16),
        pltpu.VMEM((2, SLOTS, LANES), BF16),
        pltpu.VMEM((SLOTS, TOKS), F32),
        pltpu.VMEM((SLOTS, F + LANES), BF16),
        pltpu.VMEM((Z, SLOTS, F), BF16),
        pltpu.VMEM((half, TP, 2 * F), BF16),
        pltpu.VMEM((half, TOKS, 2 * F), BF16),
        pltpu.VMEM((half, SLOTS, 2 * F), BF16),
        pltpu.VMEM((half, SLOTS, 2 * F), BF16),
        pltpu.VMEM((SLOTS, LANES), BF16),
        pltpu.VMEM((2 * HP, D), BF16),
        pltpu.VMEM((HP, D), BF16),
        pltpu.VMEM((SLOTS, 2 * HP), F32),
        pltpu.VMEM((SLOTS, HP), F32),
        pltpu.VMEM((SLOTS, 2 * HP), BF16),
        pltpu.VMEM((HP, SLOTS), BF16),
        pltpu.VMEM((4, half + 1, SLOTS // 2, A), BF16),
        pltpu.VMEM((4, half + 1, SLOTS // 2, A), BF16),
        pltpu.VMEM((half, SLOTS, F), BF16),
        pltpu.VMEM((half, SLOTS, F), BF16),
        pltpu.VMEM((half, TOKS, F), BF16),
        pltpu.VMEM((half, TOKS, F), BF16),
        pltpu.VMEM((half, TP, F), BF16),
        pltpu.VMEM((T, A), F32),
        pltpu.VMEM((Z, TP, A), BF16),
        pltpu.VMEM((Z, 8, LANES), F32),
        pltpu.VMEM((8, LANES), F32),
        pltpu.VMEM((8, LANES), F32),
        pltpu.VMEM((NP, 8, LANES), F32),
        pltpu.VMEM((SLOTS, A), BF16),
        pltpu.VMEM((SLOTS, A), BF16),
        pltpu.VMEM((TOKS, A + LANES), BF16),
        pltpu.VMEM((TOKS, A + LANES), BF16),
        pltpu.VMEM((H, D), BF16),
        dma((Y,)),
        dma((Y,)),
        dma((2, NP)),
        dma((2, NP)),
        dma((Z,)),
        dma((Z,)),
        dma((half, Y)),
        dma((half, Y)),
        dma((half, NP)),
        dma((half, NP)),
        dma((4, half)),
        dma((4, half)),
        dma((4, half + 1)),
        dma((4, half + 1)),
        dma((Z,)),
        dma((Z,)),
        dma((half, NP)),
        dma((half, NP)),
        dma((half, Y)),
        dma((half, Y)),
        dma((Z,)),
        dma((Z,)),
        dma((2, NP)),
        dma((2, NP)),
        dma((Y,)),
        dma((Y,)),
        dma((3,)),
        dma,
    ]
    grad_tokens, grad_route, grad_down = pl.pallas_call(
        functools.partial(kernel, cfg),
        out_shape=(
            jax.ShapeDtypeStruct((T, F), BF16),
            jax.ShapeDtypeStruct((T, TOP), BF16),
            jax.ShapeDtypeStruct((H, D), BF16),
        ),
        in_specs=[vmem] * 4 + [hbm] * 3,
        out_specs=(vmem, vmem, hbm),
        scratch_shapes=scratch,
        compiler_params=pltpu.CompilerParams(
            collective_id=0, has_side_effects=True, vmem_limit_bytes=60 * 1024 * 1024
        ),
        name="experts",
    )(ids, gains, tokens, grad_out, w_gate[0].T, w_up[0].T, w_down[0])
    return grad_tokens, grad_route, grad_down[None]


def solution(mesh):
    in_specs = (
        P("wide", "narrow"),
        P("wide", "narrow"),
        P("wide", None),
        P("wide", None),
        P("wide", None, "narrow"),
        P("wide", None, "narrow"),
        P("wide", "narrow", None),
    )
    out_specs = (P("wide", "narrow"), P("wide", None), P("wide", "narrow", None))
    return jax.shard_map(body, mesh=mesh, in_specs=in_specs, out_specs=out_specs, check_vma=False)
```
